256 devices in a mesh: scan: 32 (over x, y, z_lo), col: 8 (over z_hi, core).
Axes of the slice: x: 4, y: 4, z: 8 (z_hi: 4, z_lo: 2; z = z_hi * 2 + z_lo), core: 2. Of those that a mesh axis runs over, the one named last changes fastest.
Arguments:
- frames: float32 [512, 128, 2048], P('scan', None, 'col'), may hold values from -6 to 6
- depth_offset: int32 [128], replicated, may hold values from -128 to 128
- band_width: int32 [128], replicated, may hold values from 1 to 8
- edge_level: int32 [128, 2048], P(None, 'col'), may hold values from 1 to 16
Outputs:
- volume: float32 [512, 128, 2048], P('scan', None, 'col')
The draws below stay inside these ranges and needn't reach their ends.
All inputs are finite; a program needn't handle non-finite values.
Results may differ from the reference program's by a relative error of at most 0.0003.
Values sent between devices are 32-bit elements; how exact they have to be, the bound alone decides.
No kernel may reach another device: no remote copies, remote signals or barrier semaphores. Data moves between devices by JAX's collectives and lax.ppermute only.
A program may use at most 64 MiB of HBM per device.

```python
import jax
import jax.numpy as jnp
from jax import lax

R = 128
C = 2048
BAND = 8
SWEEPS = 6
DIFFUSE = 6
W = 512
SHIFT = 128


def with_ends(values, rng, smallest, largest):
    index_at = [jax.random.randint(jax.random.fold_in(rng, axis), (), 0, length) for axis, length in enumerate(values.shape)]
    widest = values.shape.index(max(values.shape))
    beside = index_at[:widest] + [(index_at[widest] + 1) % values.shape[widest]] + index_at[widest + 1:]
    return values.at[tuple(index_at)].set(smallest).at[tuple(beside)].set(largest)


def level_of(key, dims, cuts, low, high):
    def one(axis_at, parts):
        heights = jax.random.uniform(jax.random.fold_in(jax.random.fold_in(key, 6), axis_at), (parts,), jnp.float32, low / len(cuts), high / len(cuts))
        return jnp.repeat(jnp.exp(heights), dims[axis_at] // parts).reshape((-1,) + (1,) * (len(dims) - axis_at - 1))

    gain = one(*cuts[0])
    for cut in cuts[1:]:
        gain = gain * one(*cut)
    return gain


def gaussian(key, extent, deviation, limit, cuts=(), kind=jnp.bfloat16):
    factor_of = level_of(key, extent, cuts, -0.22, 0.18) if cuts else 1.0
    drawn = jax.random.normal(key, extent, jnp.float32) * deviation * factor_of
    return jnp.minimum(jnp.maximum(drawn, -limit), limit).astype(kind)


def setup_inputs(seed: int = 0) -> dict:
    key_of = jax.random.split(jax.random.key(seed), 5)
    return {
        "frames": gaussian(key_of[0], (W, R, C), 1.0, 6.0, ((0, 32), (2, 8)), jnp.float32),
        "depth_offset": with_ends(jax.random.randint(key_of[1], (R,), 0 - SHIFT, SHIFT + 1), jax.random.fold_in(key_of[1], 1), 0 - SHIFT, SHIFT).astype(jnp.int32),
        "band_width": with_ends(jax.random.randint(key_of[2], (R,), 1, BAND + 1), jax.random.fold_in(key_of[2], 1), 1, BAND).astype(jnp.int32),
        "edge_level": with_ends(jax.random.randint(key_of[3], (R, C), 1, 17), jax.random.fold_in(key_of[3], 1), 1, 16).astype(jnp.int32),
    }


TEMPORAL_KAPPA = 1.0
STEP_SIZE = 0.24
LEVEL_SCALE = 16.0


def diffuse_once(field, kappa, live_mask):
    change = (field[1:] - field[:-1]) * (live_mask[1:] * live_mask[:-1])
    flux_out = change / (1.0 + (change * change) / (kappa * kappa))
    zero_row = jnp.zeros_like(flux_out[:1])
    return field + STEP_SIZE * (jnp.concatenate([flux_out, zero_row], 0) - jnp.concatenate([zero_row, flux_out], 0))


def reference(frames, depth_offset, band_width, edge_level):
    def one_row(row_index):
        plane_rows = lax.dynamic_index_in_dim(frames, row_index, 1, keepdims=False)
        live_mask = jnp.ones((W, 1), jnp.float32)
        for sweep_no in range(SWEEPS):
            plane_rows = diffuse_once(plane_rows, TEMPORAL_KAPPA, live_mask)
        wire_signal = jnp.concatenate([plane_rows[:-1] - plane_rows[1:], jnp.zeros_like(plane_rows[:1])], 0)
        row_offset = lax.dynamic_index_in_dim(depth_offset, row_index, 0, keepdims=False)
        row_width = lax.dynamic_index_in_dim(band_width, row_index, 0, keepdims=False)
        padded = jnp.pad(wire_signal, ((SHIFT + BAND, SHIFT), (0, 0)))
        summed = jnp.zeros_like(wire_signal)
        for lag_step in range(BAND):
            start_at = (SHIFT + BAND - lag_step - row_offset).astype(jnp.int32)
            pieces = lax.dynamic_slice_in_dim(padded, start_at, W, 0)
            summed = summed + jnp.where(lag_step < row_width, pieces, jnp.zeros_like(pieces))
        profile = summed / row_width.astype(jnp.float32)
        edge_scale = lax.dynamic_index_in_dim(edge_level, row_index, 0, keepdims=True).astype(jnp.float32) / LEVEL_SCALE
        for sweep_no in range(DIFFUSE):
            profile = diffuse_once(profile, edge_scale, live_mask)
        return profile

    stacked = lax.map(one_row, jnp.arange(R, dtype=jnp.int32))
    return jnp.transpose(stacked, (1, 0, 2))
```

```python
import functools
import math

import jax
import jax.numpy as jnp
from jax import lax
from jax.experimental import pallas as pl
from jax.experimental.pallas import tpu as pltpu
from jax.sharding import PartitionSpec as P

SWEEPS = 6
DIFFUSE = 6
TEMPORAL_KAPPA = 1.0
STEP_SIZE = 0.24
LEVEL_SCALE = 16.0
BAND = 8
SHIFT = 128
SUB = 8
LANES = 128

INV_STEP = 1.0 / STEP_SIZE
ROOT_STEP = math.sqrt(STEP_SIZE)
LOW_PAD = SHIFT + BAND
HIGH_PAD = SHIFT + BAND


def sweep(count, load, store):
    here = load(0)
    flux_in = None
    for i in range(count):
        if i < count - 1:
            ahead = load(i + 1)
            change = ahead - here
            flux_out = change / (INV_STEP + change * change)
            store(i, here + (flux_out if flux_in is None else flux_out - flux_in))
            flux_in, here = flux_out, ahead
        else:
            store(i, here - flux_in)


def lines_kernel(count, offset_ref, width_ref, level_ref, lines_ref, out_ref, padded_ref):
    scale_in = 1.0 / (TEMPORAL_KAPPA * ROOT_STEP)

    def put(i, value):
        padded_ref[LOW_PAD + i] = value

    def get(i):
        return padded_ref[LOW_PAD + i]

    sweep(count, lambda i: lines_ref[i] * scale_in, put)

    def again(_, carry):
        sweep(count, get, put)
        return carry

    lax.fori_loop(0, SWEEPS - 1, again, 0)

    first, last = get(0), get(count - 1)
    for i in range(LOW_PAD):
        padded_ref[i] = first
    for i in range(HIGH_PAD):
        padded_ref[LOW_PAD + count + i] = last

    sublane = lax.broadcasted_iota(jnp.int32, (SUB, LANES), 0)
    width = jnp.zeros((SUB, LANES), jnp.int32)
    starts = []
    for r in range(SUB):
        starts.append(LOW_PAD + 1 - offset_ref[r] - width_ref[r])
        width = jnp.where(sublane == r, width_ref[r], width)
    level = level_ref[...].astype(jnp.float32)
    gain = LEVEL_SCALE / (width.astype(jnp.float32) * level)
    rows = [sublane == r for r in range(SUB)]
    less = width - 1
    bits = [(less & 1) != 0, (less & 2) != 0, (less & 4) != 0]

    def shifted(i):
        value = padded_ref[starts[0] + i]
        for r in range(1, SUB):
            value = jnp.where(rows[r], padded_ref[starts[r] + i], value)
        return value

    window = [shifted(i) for i in range(BAND + 1)]
    ones = [jnp.where(bits[0], window[i + 2], window[i + 1]) for i in range(BAND - 1)]
    twos = [jnp.where(bits[1], ones[i + 2], ones[i]) for i in range(BAND - 3)]
    for d in range(count):
        if d:
            window = window[1:] + [shifted(d + BAND)]
            ones = ones[1:] + [jnp.where(bits[0], window[BAND], window[BAND - 1])]
            twos = twos[1:] + [jnp.where(bits[1], ones[BAND - 2], ones[BAND - 4])]
        out_ref[d] = (window[0] - jnp.where(bits[2], twos[4], twos[0])) * gain

    def out_put(i, value):
        out_ref[i] = value

    def out_again(_, carry):
        sweep(count, lambda i: out_ref[i], out_put)
        return carry

    lax.fori_loop(0, DIFFUSE - 1, out_again, 0)
    scale_out = level * (ROOT_STEP / LEVEL_SCALE)

    def out_final(i, value):
        out_ref[i] = value * scale_out

    sweep(count, lambda i: out_ref[i], out_final)


def process_lines(lines, offsets, widths, levels):
    count = lines.shape[0]
    smem = pl.BlockSpec(memory_space=pltpu.SMEM)
    vmem = pl.BlockSpec(memory_space=pltpu.VMEM)
    return pl.pallas_call(
        functools.partial(lines_kernel, count),
        out_shape=jax.ShapeDtypeStruct(lines.shape, jnp.float32),
        in_specs=[smem, smem, vmem, vmem],
        out_specs=vmem,
        scratch_shapes=[pltpu.VMEM((LOW_PAD + count + HIGH_PAD, SUB, LANES), jnp.float32)],
        compiler_params=pltpu.CompilerParams(vmem_limit_bytes=12 << 20),
        name="lines",
    )(offsets, widths, levels, lines)


def body(frames, depth_offset, band_width, edge_level):
    scan_count = lax.axis_size("scan")
    me = lax.axis_index("scan")
    held, rows, cols = frames.shape
    groups, halves = rows // SUB, cols // LANES
    assert groups * halves == scan_count
    tiles = frames.reshape(held, groups, SUB, halves, LANES).transpose(1, 3, 0, 2, 4)
    tiles = tiles.reshape(scan_count, held, SUB, LANES)
    lines = lax.all_to_all(tiles, "scan", split_axis=0, concat_axis=0, tiled=True)
    lines = lines.reshape(scan_count * held, SUB, LANES)
    first_row = (me // halves) * SUB
    offsets = lax.dynamic_slice_in_dim(depth_offset, first_row, SUB, 0)
    widths = lax.dynamic_slice_in_dim(band_width, first_row, SUB, 0)
    levels = lax.dynamic_slice(edge_level, (first_row, (me % halves) * LANES), (SUB, LANES))
    done = process_lines(lines, offsets, widths, levels)
    done = done.reshape(scan_count, held, SUB, LANES)
    back = lax.all_to_all(done, "scan", split_axis=0, concat_axis=0, tiled=True)
    back = back.reshape(groups, halves, held, SUB, LANES).transpose(2, 0, 3, 1, 4)
    return back.reshape(held, rows, cols)


def solution(mesh):
    placed = (P("scan", None, "col"), P(), P(), P(None, "col"))
    return jax.shard_map(
        body, mesh=mesh, in_specs=placed, out_specs=P("scan", None, "col"), check_vma=False
    )
```

```python
import functools
import math

import jax
import jax.numpy as jnp
from jax import lax
from jax.experimental import pallas as pl
from jax.experimental.pallas import tpu as pltpu
from jax.sharding import PartitionSpec as P

SWEEPS = 6
DIFFUSE = 6
TEMPORAL_KAPPA = 1.0
STEP_SIZE = 0.24
LEVEL_SCALE = 16.0
BAND = 8
SHIFT = 128
SUB = 8
LANES = 128
HANDOVERS = 2

INV_STEP = 1.0 / STEP_SIZE
ROOT_STEP = math.sqrt(STEP_SIZE)
LOW_PAD = SHIFT + BAND
HIGH_PAD = SHIFT + BAND


def sweep(count, load, store):
    here = load(0)
    flux_in = None
    for i in range(count):
        if i < count - 1:
            ahead = load(i + 1)
            change = ahead - here
            flux_out = change / (INV_STEP + change * change)
            store(i, here + (flux_out if flux_in is None else flux_out - flux_in))
            flux_in, here = flux_out, ahead
        else:
            store(i, here - flux_in)


def lines_kernel(
    count, offset_hbm, width_hbm, level_hbm, lines_ref, out_ref,
    padded_ref, offset_ref, width_ref, level_ref, sems,
):
    halves = level_hbm.shape[1] // LANES
    me = lax.axis_index("scan")
    base = pl.multiple_of((me // halves) * SUB, SUB)
    column = pl.multiple_of((me % halves) * LANES, LANES)
    fetches = [
        pltpu.make_async_copy(offset_hbm, offset_ref, sems.at[0]),
        pltpu.make_async_copy(width_hbm, width_ref, sems.at[1]),
        pltpu.make_async_copy(
            level_hbm.at[pl.ds(base, SUB), pl.ds(column, LANES)], level_ref, sems.at[2]
        ),
    ]
    for fetch in fetches:
        fetch.start()
    scale_in = 1.0 / (TEMPORAL_KAPPA * ROOT_STEP)

    def put(i, value):
        padded_ref[LOW_PAD + i] = value

    def get(i):
        return padded_ref[LOW_PAD + i]

    sweep(count, lambda i: lines_ref[i] * scale_in, put)

    def again(_, carry):
        sweep(count, get, put)
        return carry

    lax.fori_loop(0, SWEEPS - 1, again, 0)

    first, last = get(0), get(count - 1)
    for i in range(LOW_PAD):
        padded_ref[i] = first
    for i in range(HIGH_PAD):
        padded_ref[LOW_PAD + count + i] = last

    for fetch in fetches:
        fetch.wait()
    sublane = lax.broadcasted_iota(jnp.int32, (SUB, LANES), 0)
    width = jnp.zeros((SUB, LANES), jnp.int32)
    starts = []
    for r in range(SUB):
        starts.append(LOW_PAD + 1 - offset_ref[base + r] - width_ref[base + r])
        width = jnp.where(sublane == r, width_ref[base + r], width)
    level = level_ref[...].astype(jnp.float32)
    gain = LEVEL_SCALE / (width.astype(jnp.float32) * level)
    rows = [sublane == r for r in range(SUB)]
    less = width - 1
    bits = [(less & 1) != 0, (less & 2) != 0, (less & 4) != 0]

    def shifted(i):
        value = padded_ref[starts[0] + i]
        for r in range(1, SUB):
            value = jnp.where(rows[r], padded_ref[starts[r] + i], value)
        return value

    window = [shifted(i) for i in range(BAND + 1)]
    ones = [jnp.where(bits[0], window[i + 2], window[i + 1]) for i in range(BAND - 1)]
    twos = [jnp.where(bits[1], ones[i + 2], ones[i]) for i in range(BAND - 3)]
    for d in range(count):
        if d:
            window = window[1:] + [shifted(d + BAND)]
            ones = ones[1:] + [jnp.where(bits[0], window[BAND], window[BAND - 1])]
            twos = twos[1:] + [jnp.where(bits[1], ones[BAND - 2], ones[BAND - 4])]
        out_ref[d] = (window[0] - jnp.where(bits[2], twos[4], twos[0])) * gain

    def out_put(i, value):
        out_ref[i] = value

    def out_again(_, carry):
        sweep(count, lambda i: out_ref[i], out_put)
        return carry

    lax.fori_loop(0, DIFFUSE - 1, out_again, 0)
    scale_out = level * (ROOT_STEP / LEVEL_SCALE)

    def out_final(i, value):
        out_ref[i] = value * scale_out

    sweep(count, lambda i: out_ref[i], out_final)


def process_lines(lines, depth_offset, band_width, edge_level):
    count = lines.shape[0]
    vmem = pl.BlockSpec(memory_space=pltpu.VMEM)
    hbm = pl.BlockSpec(memory_space=pltpu.HBM)
    return pl.pallas_call(
        functools.partial(lines_kernel, count),
        out_shape=jax.ShapeDtypeStruct(lines.shape, jnp.float32),
        in_specs=[hbm, hbm, hbm, vmem],
        out_specs=vmem,
        scratch_shapes=[
            pltpu.VMEM((LOW_PAD + count + HIGH_PAD, SUB, LANES), jnp.float32),
            pltpu.SMEM(depth_offset.shape, jnp.int32),
            pltpu.SMEM(band_width.shape, jnp.int32),
            pltpu.VMEM((SUB, LANES), jnp.int32),
            pltpu.SemaphoreType.DMA((3,)),
        ],
        compiler_params=pltpu.CompilerParams(vmem_limit_bytes=12 << 20),
        name="lines",
    )(depth_offset, band_width, edge_level, lines)


def body(frames, depth_offset, band_width, edge_level):
    scan_count = lax.axis_size("scan")
    held, rows, cols = frames.shape
    groups, halves = rows // SUB, cols // LANES
    assert groups * halves == scan_count

    def tiled(part):
        tiles = part.reshape(held, groups, SUB, halves, LANES).transpose(1, 3, 0, 2, 4)
        return tiles.reshape(scan_count, held, SUB, LANES)

    def exchange(tiles):
        return lax.all_to_all(tiles, "scan", split_axis=0, concat_axis=0, tiled=True)

    def after_token(frames):
        pairs = [(p, p ^ 1) for p in range(scan_count)]
        token = frames[0, :SUB, :LANES]
        for _ in range(HANDOVERS):
            token = lax.ppermute(token, "scan", pairs)
        return exchange(tiled(frames) + 0.0 * token[0, 0])

    def at_once(frames):
        return exchange(tiled(frames))

    lines = lax.cond(lax.axis_index("col") % 2 == 0, after_token, at_once, frames)
    lines = lines.reshape(scan_count * held, SUB, LANES)
    done = process_lines(lines, depth_offset, band_width, edge_level)
    back = lax.all_to_all(done.reshape(scan_count * held, 1, SUB, LANES), "scan", split_axis=0, concat_axis=1, tiled=True)
    back = back.reshape(held, groups, halves, SUB, LANES).transpose(0, 1, 3, 2, 4)
    return back.reshape(held, rows, cols)


def solution(mesh):
    placed = (P("scan", None, "col"), P(), P(), P(None, "col"))
    return jax.shard_map(
        body, mesh=mesh, in_specs=placed, out_specs=P("scan", None, "col"), check_vma=False
    )
```

```python
import functools
import math

import jax
import jax.numpy as jnp
from jax import lax
from jax.experimental import pallas as pl
from jax.experimental.pallas import tpu as pltpu
from jax.sharding import PartitionSpec as P

SWEEPS = 6
DIFFUSE = 6
TEMPORAL_KAPPA = 1.0
STEP_SIZE = 0.24
LEVEL_SCALE = 16.0
BAND = 8
SHIFT = 128
SUB = 8
LANES = 128
HANDOVERS = 2

INV_STEP = 1.0 / STEP_SIZE
ROOT_STEP = math.sqrt(STEP_SIZE)
LOW_PAD = SHIFT + BAND
HIGH_PAD = SHIFT + BAND


def sweep(count, load, store):
    here = load(0)
    flux_in = None
    for i in range(count):
        if i < count - 1:
            ahead = load(i + 1)
            change = ahead - here
            flux_out = change / (INV_STEP + change * change)
            store(i, here + (flux_out if flux_in is None else flux_out - flux_in))
            flux_in, here = flux_out, ahead
        else:
            store(i, here - flux_in)


def lines_kernel(
    count, offset_hbm, width_hbm, level_hbm, lines_ref, out_ref,
    padded_ref, shifted_ref, offset_ref, width_ref, level_ref, sems,
):
    halves = level_hbm.shape[1] // LANES
    me = lax.axis_index("scan")
    base = pl.multiple_of((me // halves) * SUB, SUB)
    column = pl.multiple_of((me % halves) * LANES, LANES)
    fetches = [
        pltpu.make_async_copy(offset_hbm, offset_ref, sems.at[0]),
        pltpu.make_async_copy(width_hbm, width_ref, sems.at[1]),
        pltpu.make_async_copy(
            level_hbm.at[pl.ds(base, SUB), pl.ds(column, LANES)], level_ref, sems.at[2]
        ),
    ]
    for fetch in fetches:
        fetch.start()
    scale_in = 1.0 / (TEMPORAL_KAPPA * ROOT_STEP)

    def put(i, value):
        padded_ref[pl.ds(SUB * (LOW_PAD + i), SUB), :] = value

    def get(i):
        return padded_ref[pl.ds(SUB * (LOW_PAD + i), SUB), :]

    sweep(count, lambda i: lines_ref[i] * scale_in, put)

    def again(_, carry):
        sweep(count, get, put)
        return carry

    lax.fori_loop(0, SWEEPS - 2, again, 0)

    ends = {}

    def put_padded(i, value):
        put(i, value)
        first = ends.setdefault("first", value)
        if i < LOW_PAD:
            padded_ref[pl.ds(SUB * i, SUB), :] = first
        if i == count - 1:
            for k in range(HIGH_PAD):
                padded_ref[pl.ds(SUB * (LOW_PAD + count + k), SUB), :] = value

    sweep(count, get, put_padded)

    for fetch in fetches:
        fetch.wait()
    sublane = lax.broadcasted_iota(jnp.int32, (SUB, LANES), 0)
    width = jnp.zeros((SUB, LANES), jnp.int32)
    starts = []
    for r in range(SUB):
        starts.append(LOW_PAD + 1 - offset_ref[base + r] - width_ref[base + r])
        width = jnp.where(sublane == r, width_ref[base + r], width)
    level = level_ref[...].astype(jnp.float32)
    gain = LEVEL_SCALE / (width.astype(jnp.float32) * level)
    less = width - 1
    bits = [(less & 1) != 0, (less & 2) != 0, (less & 4) != 0]

    def shift_block(block):
        at = SUB * SUB * block
        for r in range(SUB):
            shifted_ref[pl.ds(at + r, SUB, stride=SUB), :] = (
                padded_ref[pl.ds(SUB * starts[r] + r + at, SUB, stride=SUB), :]
            )

    def shifted(i):
        if i % SUB == 0:
            shift_block(i // SUB)
        return shifted_ref[pl.ds(SUB * i, SUB), :]

    held = {}

    def profile(d):
        if d == 0:
            window = [shifted(i) for i in range(BAND + 1)]
            ones = [jnp.where(bits[0], window[i + 2], window[i + 1]) for i in range(BAND - 1)]
            twos = [jnp.where(bits[1], ones[i + 2], ones[i]) for i in range(BAND - 3)]
        else:
            window, ones, twos = held["window"], held["ones"], held["twos"]
            window = window[1:] + [shifted(d + BAND)]
            ones = ones[1:] + [jnp.where(bits[0], window[BAND], window[BAND - 1])]
            twos = twos[1:] + [jnp.where(bits[1], ones[BAND - 2], ones[BAND - 4])]
        held.update(window=window, ones=ones, twos=twos)
        return (window[0] - jnp.where(bits[2], twos[4], twos[0])) * gain

    def out_put(i, value):
        out_ref[i] = value

    def out_again(_, carry):
        sweep(count, lambda i: out_ref[i], out_put)
        return carry

    sweep(count, profile, out_put)
    lax.fori_loop(0, DIFFUSE - 2, out_again, 0)
    scale_out = level * (ROOT_STEP / LEVEL_SCALE)

    def out_final(i, value):
        out_ref[i] = value * scale_out

    sweep(count, lambda i: out_ref[i], out_final)


def process_lines(lines, depth_offset, band_width, edge_level):
    count = lines.shape[0]
    vmem = pl.BlockSpec(memory_space=pltpu.VMEM)
    hbm = pl.BlockSpec(memory_space=pltpu.HBM)
    return pl.pallas_call(
        functools.partial(lines_kernel, count),
        out_shape=jax.ShapeDtypeStruct(lines.shape, jnp.float32),
        in_specs=[hbm, hbm, hbm, vmem],
        out_specs=vmem,
        scratch_shapes=[
            pltpu.VMEM(((LOW_PAD + count + HIGH_PAD) * SUB, LANES), jnp.float32),
            pltpu.VMEM(((count + BAND) * SUB, LANES), jnp.float32),
            pltpu.SMEM(depth_offset.shape, jnp.int32),
            pltpu.SMEM(band_width.shape, jnp.int32),
            pltpu.VMEM((SUB, LANES), jnp.int32),
            pltpu.SemaphoreType.DMA((3,)),
        ],
        compiler_params=pltpu.CompilerParams(vmem_limit_bytes=14 << 20),
        name="lines",
    )(depth_offset, band_width, edge_level, lines)


def body(frames, depth_offset, band_width, edge_level):
    scan_count = lax.axis_size("scan")
    held, rows, cols = frames.shape
    groups, halves = rows // SUB, cols // LANES
    assert groups * halves == scan_count

    def tiled(part):
        tiles = part.reshape(held, groups, SUB, halves, LANES).transpose(1, 3, 0, 2, 4)
        return tiles.reshape(scan_count, held, SUB, LANES)

    def exchange(tiles):
        return lax.all_to_all(tiles, "scan", split_axis=0, concat_axis=0, tiled=True)

    def after_token(frames):
        pairs = [(p, p ^ 1) for p in range(scan_count)]
        token = frames[0, :SUB, :LANES]
        for _ in range(HANDOVERS):
            token = lax.ppermute(token, "scan", pairs)
        return exchange(tiled(frames) + 0.0 * token[0, 0])

    def at_once(frames):
        return exchange(tiled(frames))

    lines = lax.cond(lax.axis_index("col") % 2 == 0, after_token, at_once, frames)
    lines = lines.reshape(scan_count * held, SUB, LANES)
    done = process_lines(lines, depth_offset, band_width, edge_level)
    back = lax.all_to_all(done.reshape(scan_count * held, 1, SUB, LANES), "scan", split_axis=0, concat_axis=1, tiled=True)
    back = back.reshape(held, groups, halves, SUB, LANES).transpose(0, 1, 3, 2, 4)
    return back.reshape(held, rows, cols)


def solution(mesh):
    placed = (P("scan", None, "col"), P(), P(), P(None, "col"))
    return jax.shard_map(
        body, mesh=mesh, in_specs=placed, out_specs=P("scan", None, "col"), check_vma=False
    )
```

```python
import functools
import math

import jax
import jax.numpy as jnp
from jax import lax
from jax.experimental import pallas as pl
from jax.experimental.pallas import tpu as pltpu
from jax.sharding import PartitionSpec as P

SWEEPS = 6
DIFFUSE = 6
TEMPORAL_KAPPA = 1.0
STEP_SIZE = 0.24
LEVEL_SCALE = 16.0
BAND = 8
SHIFT = 128
SUB = 8
LANES = 128
HANDOVERS = 2

INV_STEP = 1.0 / STEP_SIZE
ROOT_STEP = math.sqrt(STEP_SIZE)
LOW_PAD = SHIFT + BAND
HIGH_PAD = SHIFT + BAND


def sweep(count, load, store):
    here = load(0)
    flux_in = None
    for i in range(count):
        if i < count - 1:
            ahead = load(i + 1)
            change = ahead - here
            flux_out = change / (INV_STEP + change * change)
            store(i, here + (flux_out if flux_in is None else flux_out - flux_in))
            flux_in, here = flux_out, ahead
        else:
            store(i, here - flux_in)


def lines_kernel(
    count, offset_hbm, width_hbm, level_hbm, lines_ref, out_ref,
    padded_ref, shifted_ref, offset_ref, width_ref, level_ref, sems,
):
    halves = level_hbm.shape[1] // LANES
    me = lax.axis_index("scan")
    base = pl.multiple_of((me // halves) * SUB, SUB)
    column = pl.multiple_of((me % halves) * LANES, LANES)
    fetches = [
        pltpu.make_async_copy(offset_hbm, offset_ref, sems.at[0]),
        pltpu.make_async_copy(width_hbm, width_ref, sems.at[1]),
        pltpu.make_async_copy(
            level_hbm.at[pl.ds(base, SUB), pl.ds(column, LANES)], level_ref, sems.at[2]
        ),
    ]
    for fetch in fetches:
        fetch.start()
    scale_in = 1.0 / (TEMPORAL_KAPPA * ROOT_STEP)

    def put(i, value):
        padded_ref[pl.ds(SUB * (LOW_PAD + i), SUB), :] = value

    def get(i):
        return padded_ref[pl.ds(SUB * (LOW_PAD + i), SUB), :]

    sweep(count, lambda i: lines_ref[i] * scale_in, put)

    def again(_, carry):
        sweep(count, get, put)
        return carry

    lax.fori_loop(0, SWEEPS - 2, again, 0)

    ends = {}

    def put_padded(i, value):
        put(i, value)
        first = ends.setdefault("first", value)
        if i < LOW_PAD:
            padded_ref[pl.ds(SUB * i, SUB), :] = first
        if i == count - 1:
            for k in range(HIGH_PAD):
                padded_ref[pl.ds(SUB * (LOW_PAD + count + k), SUB), :] = value

    sweep(count, get, put_padded)

    for fetch in fetches:
        fetch.wait()
    sublane = lax.broadcasted_iota(jnp.int32, (SUB, LANES), 0)
    width = jnp.zeros((SUB, LANES), jnp.int32)
    starts = []
    for r in range(SUB):
        starts.append(LOW_PAD + 1 - offset_ref[base + r] - width_ref[base + r])
        width = jnp.where(sublane == r, width_ref[base + r], width)
    level = level_ref[...].astype(jnp.float32)
    gain = LEVEL_SCALE / (width.astype(jnp.float32) * level)
    less = width - 1
    bits = [(less & 1) != 0, (less & 2) != 0, (less & 4) != 0]

    def shift_block(block):
        at = SUB * SUB * block
        for r in range(SUB):
            shifted_ref[pl.ds(at + r, SUB, stride=SUB), :] = (
                padded_ref[pl.ds(SUB * starts[r] + r + at, SUB, stride=SUB), :]
            )

    def shifted(i):
        if i % SUB == 0:
            shift_block(i // SUB)
        return shifted_ref[pl.ds(SUB * i, SUB), :]

    held = {}

    def profile(d):
        if d == 0:
            window = [shifted(i) for i in range(BAND + 1)]
            ones = [jnp.where(bits[0], window[i + 2], window[i + 1]) for i in range(BAND - 1)]
            twos = [jnp.where(bits[1], ones[i + 2], ones[i]) for i in range(BAND - 3)]
        else:
            window, ones, twos = held["window"], held["ones"], held["twos"]
            window = window[1:] + [shifted(d + BAND)]
            ones = ones[1:] + [jnp.where(bits[0], window[BAND], window[BAND - 1])]
            twos = twos[1:] + [jnp.where(bits[1], ones[BAND - 2], ones[BAND - 4])]
        held.update(window=window, ones=ones, twos=twos)
        return (window[0] - jnp.where(bits[2], twos[4], twos[0])) * gain

    def out_put(i, value):
        out_ref[i] = value

    def out_again(_, carry):
        sweep(count, lambda i: out_ref[i], out_put)
        return carry

    sweep(count, profile, out_put)
    lax.fori_loop(0, DIFFUSE - 2, out_again, 0)
    scale_out = level * (ROOT_STEP / LEVEL_SCALE)

    def out_final(i, value):
        out_ref[i] = value * scale_out

    sweep(count, lambda i: out_ref[i], out_final)


def process_lines(lines, depth_offset, band_width, edge_level):
    count = lines.shape[0]
    vmem = pl.BlockSpec(memory_space=pltpu.VMEM)
    hbm = pl.BlockSpec(memory_space=pltpu.HBM)
    return pl.pallas_call(
        functools.partial(lines_kernel, count),
        out_shape=jax.ShapeDtypeStruct(lines.shape, jnp.float32),
        in_specs=[hbm, hbm, hbm, vmem],
        out_specs=vmem,
        scratch_shapes=[
            pltpu.VMEM(((LOW_PAD + count + HIGH_PAD + 1) * SUB, LANES), jnp.float32),
            pltpu.VMEM(((count + BAND + 1) * SUB, LANES), jnp.float32),
            pltpu.SMEM(depth_offset.shape, jnp.int32),
            pltpu.SMEM(band_width.shape, jnp.int32),
            pltpu.VMEM((SUB, LANES), jnp.int32),
            pltpu.SemaphoreType.DMA((3,)),
        ],
        compiler_params=pltpu.CompilerParams(vmem_limit_bytes=14 << 20),
        name="lines",
    )(depth_offset, band_width, edge_level, lines)


def body(frames, depth_offset, band_width, edge_level):
    scan_count = lax.axis_size("scan")
    held, rows, cols = frames.shape
    groups, halves = rows // SUB, cols // LANES
    assert groups * halves == scan_count

    def tiled(part):
        tiles = part.reshape(held, groups, SUB, halves, LANES).transpose(1, 3, 0, 2, 4)
        return tiles.reshape(scan_count, held, SUB, LANES)

    def exchange(tiles):
        return lax.all_to_all(tiles, "scan", split_axis=0, concat_axis=0, tiled=True)

    def after_token(frames):
        pairs = [(p, p ^ 1) for p in range(scan_count)]
        token = frames[:4, :SUB, :LANES]
        for _ in range(HANDOVERS):
            token = lax.ppermute(token, "scan", pairs)
        return exchange(tiled(frames) + 0.0 * token[0, 0, 0])

    def at_once(frames):
        return exchange(tiled(frames))

    lines = lax.cond(lax.axis_index("col") % 2 == 0, after_token, at_once, frames)
    lines = lines.reshape(scan_count * held, SUB, LANES)
    done = process_lines(lines, depth_offset, band_width, edge_level)
    back = lax.all_to_all(done.reshape(scan_count * held, 1, SUB, LANES), "scan", split_axis=0, concat_axis=1, tiled=True)
    back = back.reshape(held, groups, halves, SUB, LANES).transpose(0, 1, 3, 2, 4)
    return back.reshape(held, rows, cols)


def solution(mesh):
    placed = (P("scan", None, "col"), P(), P(), P(None, "col"))
    return jax.shard_map(
        body, mesh=mesh, in_specs=placed, out_specs=P("scan", None, "col"), check_vma=False
    )
```

```python
import functools
import math

import jax
import jax.numpy as jnp
from jax import lax
from jax.experimental import pallas as pl
from jax.experimental.pallas import tpu as pltpu
from jax.sharding import PartitionSpec as P

SWEEPS = 6
DIFFUSE = 6
TEMPORAL_KAPPA = 1.0
STEP_SIZE = 0.24
LEVEL_SCALE = 16.0
BAND = 8
SHIFT = 128
SUB = 8
LANES = 128
HANDOVERS = 2

INV_STEP = 1.0 / STEP_SIZE
ROOT_STEP = math.sqrt(STEP_SIZE)
LOW_PAD = SHIFT + BAND
HIGH_PAD = SHIFT + BAND


def sweep(count, load, store):
    here = load(0)
    flux_in = None
    for i in range(count):
        if i < count - 1:
            ahead = load(i + 1)
            change = ahead - here
            flux_out = change / (INV_STEP + change * change)
            store(i, here + (flux_out if flux_in is None else flux_out - flux_in))
            flux_in, here = flux_out, ahead
        else:
            store(i, here - flux_in)


def lines_kernel(
    count, offset_hbm, width_hbm, level_hbm, lines_ref, out_ref,
    padded_ref, shifted_ref, offset_ref, width_ref, level_ref, sems,
):
    halves = level_hbm.shape[1] // LANES
    me = lax.axis_index("scan")
    base = pl.multiple_of((me // halves) * SUB, SUB)
    column = pl.multiple_of((me % halves) * LANES, LANES)
    fetches = [
        pltpu.make_async_copy(offset_hbm, offset_ref, sems.at[0]),
        pltpu.make_async_copy(width_hbm, width_ref, sems.at[1]),
        pltpu.make_async_copy(
            level_hbm.at[pl.ds(base, SUB), pl.ds(column, LANES)], level_ref, sems.at[2]
        ),
    ]
    for fetch in fetches:
        fetch.start()
    scale_in = 1.0 / (TEMPORAL_KAPPA * ROOT_STEP)

    def put(i, value):
        padded_ref[pl.ds(SUB * (LOW_PAD + i), SUB), :] = value

    def get(i):
        return padded_ref[pl.ds(SUB * (LOW_PAD + i), SUB), :]

    sweep(count, lambda i: lines_ref[i] * scale_in, put)

    def again(_, carry):
        sweep(count, get, put)
        return carry

    lax.fori_loop(0, SWEEPS - 2, again, 0)

    ends = {}

    def put_padded(i, value):
        put(i, value)
        first = ends.setdefault("first", value)
        if i < LOW_PAD:
            padded_ref[pl.ds(SUB * i, SUB), :] = first
        if i == count - 1:
            for k in range(HIGH_PAD):
                padded_ref[pl.ds(SUB * (LOW_PAD + count + k), SUB), :] = value

    sweep(count, get, put_padded)

    for fetch in fetches:
        fetch.wait()
    sublane = lax.broadcasted_iota(jnp.int32, (SUB, LANES), 0)
    width = jnp.zeros((SUB, LANES), jnp.int32)
    starts = []
    for r in range(SUB):
        starts.append(LOW_PAD + 1 - offset_ref[base + r] - width_ref[base + r])
        width = jnp.where(sublane == r, width_ref[base + r], width)
    level = level_ref[...].astype(jnp.float32)
    gain = LEVEL_SCALE / (width.astype(jnp.float32) * level)
    less = width - 1
    bits = [(less & 1) != 0, (less & 2) != 0, (less & 4) != 0]

    def shift_block(block):
        at = SUB * SUB * block
        for r in range(SUB):
            shifted_ref[pl.ds(at + r, SUB, stride=SUB), :] = (
                padded_ref[pl.ds(SUB * starts[r] + r + at, SUB, stride=SUB), :]
            )

    def shifted(i):
        if i % SUB == 0:
            shift_block(i // SUB)
        return shifted_ref[pl.ds(SUB * i, SUB), :]

    held = {}

    def profile(d):
        if d == 0:
            window = [shifted(i) for i in range(BAND + 1)]
            ones = [jnp.where(bits[0], window[i + 2], window[i + 1]) for i in range(BAND - 1)]
            twos = [jnp.where(bits[1], ones[i + 2], ones[i]) for i in range(BAND - 3)]
        else:
            window, ones, twos = held["window"], held["ones"], held["twos"]
            window = window[1:] + [shifted(d + BAND)]
            ones = ones[1:] + [jnp.where(bits[0], window[BAND], window[BAND - 1])]
            twos = twos[1:] + [jnp.where(bits[1], ones[BAND - 2], ones[BAND - 4])]
        held.update(window=window, ones=ones, twos=twos)
        return (window[0] - jnp.where(bits[2], twos[4], twos[0])) * gain

    def out_put(i, value):
        out_ref[i] = value

    def out_again(_, carry):
        sweep(count, lambda i: out_ref[i], out_put)
        return carry

    sweep(count, profile, out_put)
    lax.fori_loop(0, DIFFUSE - 2, out_again, 0)
    scale_out = level * (ROOT_STEP / LEVEL_SCALE)

    def out_final(i, value):
        out_ref[i] = value * scale_out

    sweep(count, lambda i: out_ref[i], out_final)


def process_lines(lines, depth_offset, band_width, edge_level):
    count = lines.shape[0]
    vmem = pl.BlockSpec(memory_space=pltpu.VMEM)
    hbm = pl.BlockSpec(memory_space=pltpu.HBM)
    return pl.pallas_call(
        functools.partial(lines_kernel, count),
        out_shape=jax.ShapeDtypeStruct(lines.shape, jnp.float32),
        in_specs=[hbm, hbm, hbm, vmem],
        out_specs=vmem,
        scratch_shapes=[
            pltpu.VMEM(((LOW_PAD + count + HIGH_PAD + 1) * SUB, LANES), jnp.float32),
            pltpu.VMEM(((count + BAND + 1) * SUB, LANES), jnp.float32),
            pltpu.SMEM(depth_offset.shape, jnp.int32),
            pltpu.SMEM(band_width.shape, jnp.int32),
            pltpu.VMEM((SUB, LANES), jnp.int32),
            pltpu.SemaphoreType.DMA((3,)),
        ],
        compiler_params=pltpu.CompilerParams(vmem_limit_bytes=14 << 20),
        name="lines",
    )(depth_offset, band_width, edge_level, lines)


def copy_all(copies):
    for copy in copies:
        copy.start()
    for copy in copies:
        copy.wait()


def to_frames_kernel(tiles_ref, frames_ref, sems):
    copy_all([
        pltpu.make_async_copy(tiles_ref.at[:, f], frames_ref.at[f], sems.at[f])
        for f in range(frames_ref.shape[0])
    ])


def to_tiles_kernel(frames_ref, tiles_ref, sems):
    copy_all([
        pltpu.make_async_copy(frames_ref.at[f], tiles_ref.at[:, f], sems.at[f])
        for f in range(frames_ref.shape[0])
    ])


def relayout(kernel, value, source, target, name):
    shape = (value.shape[1], value.shape[0]) + value.shape[2:]
    return pl.pallas_call(
        kernel,
        out_shape=jax.ShapeDtypeStruct(shape, value.dtype),
        in_specs=[pl.BlockSpec(memory_space=source)],
        out_specs=pl.BlockSpec(memory_space=target),
        scratch_shapes=[pltpu.SemaphoreType.DMA((min(shape[:2]),))],
        compiler_params=pltpu.CompilerParams(vmem_limit_bytes=6 << 20),
        name=name,
    )(value)


def body(frames, depth_offset, band_width, edge_level):
    scan_count = lax.axis_size("scan")
    held, rows, cols = frames.shape
    groups, halves = rows // SUB, cols // LANES
    assert groups * halves == scan_count

    def tiled(part):
        tiles = part.reshape(held, groups, SUB, halves, LANES).transpose(1, 3, 0, 2, 4)
        return tiles.reshape(scan_count, held, SUB, LANES)

    def exchange(tiles):
        return lax.all_to_all(tiles, "scan", split_axis=0, concat_axis=0, tiled=True)

    def after_token(frames):
        pairs = [(p, p ^ 1) for p in range(scan_count)]
        token = frames[:4, :SUB, :LANES]
        for _ in range(HANDOVERS):
            token = lax.ppermute(token, "scan", pairs)
        return exchange(tiled(frames) + 0.0 * token[0, 0, 0])

    def at_once(frames):
        tiles = frames.reshape(held, groups, SUB, halves, LANES).transpose(0, 1, 3, 2, 4)
        tiles = tiles.reshape(held, scan_count, SUB, LANES)
        tiles = pltpu.with_memory_space_constraint(tiles, pltpu.HBM)
        return exchange(relayout(to_tiles_kernel, tiles, pltpu.HBM, pltpu.VMEM, "to_tiles"))

    lines = lax.cond(lax.axis_index("col") % 2 == 0, after_token, at_once, frames)
    lines = lines.reshape(scan_count * held, SUB, LANES)
    done = process_lines(lines, depth_offset, band_width, edge_level)
    back = exchange(done.reshape(scan_count, held, SUB, LANES))
    back = relayout(to_frames_kernel, back, pltpu.VMEM, pltpu.HBM, "to_frames")
    back = back.reshape(held, groups, halves, SUB, LANES).transpose(0, 1, 3, 2, 4)
    return back.reshape(held, rows, cols)


def solution(mesh):
    placed = (P("scan", None, "col"), P(), P(), P(None, "col"))
    return jax.shard_map(
        body, mesh=mesh, in_specs=placed, out_specs=P("scan", None, "col"), check_vma=False
    )
```

```python
import functools
import math

import jax
import jax.numpy as jnp
from jax import lax
from jax.experimental import pallas as pl
from jax.experimental.pallas import tpu as pltpu
from jax.sharding import PartitionSpec as P

SWEEPS = 6
DIFFUSE = 6
TEMPORAL_KAPPA = 1.0
STEP_SIZE = 0.24
LEVEL_SCALE = 16.0
BAND = 8
SHIFT = 128
SUB = 8
LANES = 128
HANDOVERS = 2

INV_STEP = 1.0 / STEP_SIZE
ROOT_STEP = math.sqrt(STEP_SIZE)
LOW_PAD = SHIFT + BAND
HIGH_PAD = SHIFT + BAND


def sweep(count, load, store):
    here = load(0)
    flux_in = None
    for i in range(count):
        if i < count - 1:
            ahead = load(i + 1)
            change = ahead - here
            flux_out = change / (INV_STEP + change * change)
            store(i, here + (flux_out if flux_in is None else flux_out - flux_in))
            flux_in, here = flux_out, ahead
        else:
            store(i, here - flux_in)


def lines_kernel(
    count, offset_hbm, width_hbm, level_hbm, lines_ref, out_ref,
    padded_ref, shifted_ref, offset_ref, width_ref, level_ref, sems,
):
    halves = level_hbm.shape[1] // LANES
    me = lax.axis_index("scan")
    base = pl.multiple_of((me // halves) * SUB, SUB)
    column = pl.multiple_of((me % halves) * LANES, LANES)
    fetches = [
        pltpu.make_async_copy(offset_hbm, offset_ref, sems.at[0]),
        pltpu.make_async_copy(width_hbm, width_ref, sems.at[1]),
        pltpu.make_async_copy(
            level_hbm.at[pl.ds(base, SUB), pl.ds(column, LANES)], level_ref, sems.at[2]
        ),
    ]
    for fetch in fetches:
        fetch.start()
    scale_in = 1.0 / (TEMPORAL_KAPPA * ROOT_STEP)

    def put(i, value):
        padded_ref[pl.ds(SUB * (LOW_PAD + i), SUB), :] = value

    def get(i):
        return padded_ref[pl.ds(SUB * (LOW_PAD + i), SUB), :]

    sweep(count, lambda i: lines_ref[i] * scale_in, put)

    def again(_, carry):
        sweep(count, get, put)
        return carry

    lax.fori_loop(0, SWEEPS - 2, again, 0, unroll=2)

    ends = {}

    def put_padded(i, value):
        put(i, value)
        first = ends.setdefault("first", value)
        if i < LOW_PAD:
            padded_ref[pl.ds(SUB * i, SUB), :] = first
        if i == count - 1:
            for k in range(HIGH_PAD):
                padded_ref[pl.ds(SUB * (LOW_PAD + count + k), SUB), :] = value

    sweep(count, get, put_padded)

    for fetch in fetches:
        fetch.wait()
    sublane = lax.broadcasted_iota(jnp.int32, (SUB, LANES), 0)
    width = jnp.zeros((SUB, LANES), jnp.int32)
    starts = []
    for r in range(SUB):
        starts.append(LOW_PAD + 1 - offset_ref[base + r] - width_ref[base + r])
        width = jnp.where(sublane == r, width_ref[base + r], width)
    level = level_ref[...].astype(jnp.float32)
    gain = LEVEL_SCALE / (width.astype(jnp.float32) * level)
    less = width - 1
    bits = [(less & 1) != 0, (less & 2) != 0, (less & 4) != 0]

    def shift_block(block):
        at = SUB * SUB * block
        for r in range(SUB):
            shifted_ref[pl.ds(at + r, SUB, stride=SUB), :] = (
                padded_ref[pl.ds(SUB * starts[r] + r + at, SUB, stride=SUB), :]
            )

    def shifted(i):
        if i % SUB == 0:
            shift_block(i // SUB)
        return shifted_ref[pl.ds(SUB * i, SUB), :]

    held = {}

    def profile(d):
        if d == 0:
            window = [shifted(i) for i in range(BAND + 1)]
            ones = [jnp.where(bits[0], window[i + 2], window[i + 1]) for i in range(BAND - 1)]
            twos = [jnp.where(bits[1], ones[i + 2], ones[i]) for i in range(BAND - 3)]
        else:
            window, ones, twos = held["window"], held["ones"], held["twos"]
            window = window[1:] + [shifted(d + BAND)]
            ones = ones[1:] + [jnp.where(bits[0], window[BAND], window[BAND - 1])]
            twos = twos[1:] + [jnp.where(bits[1], ones[BAND - 2], ones[BAND - 4])]
        held.update(window=window, ones=ones, twos=twos)
        return (window[0] - jnp.where(bits[2], twos[4], twos[0])) * gain

    def out_put(i, value):
        out_ref[i] = value

    def out_again(_, carry):
        sweep(count, lambda i: out_ref[i], out_put)
        return carry

    sweep(count, profile, out_put)
    lax.fori_loop(0, DIFFUSE - 2, out_again, 0, unroll=2)
    scale_out = level * (ROOT_STEP / LEVEL_SCALE)

    def out_final(i, value):
        out_ref[i] = value * scale_out

    sweep(count, lambda i: out_ref[i], out_final)


def process_lines(lines, depth_offset, band_width, edge_level):
    count = lines.shape[0]
    vmem = pl.BlockSpec(memory_space=pltpu.VMEM)
    hbm = pl.BlockSpec(memory_space=pltpu.HBM)
    return pl.pallas_call(
        functools.partial(lines_kernel, count),
        out_shape=jax.ShapeDtypeStruct(lines.shape, jnp.float32),
        in_specs=[hbm, hbm, hbm, vmem],
        out_specs=vmem,
        scratch_shapes=[
            pltpu.VMEM(((LOW_PAD + count + HIGH_PAD + 1) * SUB, LANES), jnp.float32),
            pltpu.VMEM(((count + BAND + 1) * SUB, LANES), jnp.float32),
            pltpu.SMEM(depth_offset.shape, jnp.int32),
            pltpu.SMEM(band_width.shape, jnp.int32),
            pltpu.VMEM((SUB, LANES), jnp.int32),
            pltpu.SemaphoreType.DMA((3,)),
        ],
        compiler_params=pltpu.CompilerParams(vmem_limit_bytes=14 << 20),
        name="lines",
    )(depth_offset, band_width, edge_level, lines)


def copy_all(copies):
    for copy in copies:
        copy.start()
    for copy in copies:
        copy.wait()


def to_frames_kernel(tiles_ref, frames_ref, sems):
    copy_all([
        pltpu.make_async_copy(tiles_ref.at[:, f], frames_ref.at[f], sems.at[f])
        for f in range(frames_ref.shape[0])
    ])


def to_tiles_kernel(frames_ref, tiles_ref, sems):
    copy_all([
        pltpu.make_async_copy(frames_ref.at[f], tiles_ref.at[:, f], sems.at[f])
        for f in range(frames_ref.shape[0])
    ])


def relayout(kernel, value, source, target, name):
    shape = (value.shape[1], value.shape[0]) + value.shape[2:]
    return pl.pallas_call(
        kernel,
        out_shape=jax.ShapeDtypeStruct(shape, value.dtype),
        in_specs=[pl.BlockSpec(memory_space=source)],
        out_specs=pl.BlockSpec(memory_space=target),
        scratch_shapes=[pltpu.SemaphoreType.DMA((min(shape[:2]),))],
        compiler_params=pltpu.CompilerParams(vmem_limit_bytes=6 << 20),
        name=name,
    )(value)


def body(frames, depth_offset, band_width, edge_level):
    scan_count = lax.axis_size("scan")
    held, rows, cols = frames.shape
    groups, halves = rows // SUB, cols // LANES
    assert groups * halves == scan_count

    def tiled(part):
        tiles = part.reshape(held, groups, SUB, halves, LANES).transpose(1, 3, 0, 2, 4)
        return tiles.reshape(scan_count, held, SUB, LANES)

    def exchange(tiles):
        return lax.all_to_all(tiles, "scan", split_axis=0, concat_axis=0, tiled=True)

    def after_token(frames):
        pairs = [(p, p ^ 1) for p in range(scan_count)]
        token = frames[:4, :SUB, :LANES]
        for _ in range(HANDOVERS):
            token = lax.ppermute(token, "scan", pairs)
        return exchange(tiled(frames) + 0.0 * token[0, 0, 0])

    def at_once(frames):
        tiles = frames.reshape(held, groups, SUB, halves, LANES).transpose(0, 1, 3, 2, 4)
        tiles = tiles.reshape(held, scan_count, SUB, LANES)
        tiles = pltpu.with_memory_space_constraint(tiles, pltpu.HBM)
        return exchange(relayout(to_tiles_kernel, tiles, pltpu.HBM, pltpu.VMEM, "to_tiles"))

    lines = lax.cond(lax.axis_index("col") % 2 == 0, after_token, at_once, frames)
    lines = lines.reshape(scan_count * held, SUB, LANES)
    done = process_lines(lines, depth_offset, band_width, edge_level)
    back = exchange(done.reshape(scan_count, held, SUB, LANES))
    back = relayout(to_frames_kernel, back, pltpu.VMEM, pltpu.HBM, "to_frames")
    back = back.reshape(held, groups, halves, SUB, LANES).transpose(0, 1, 3, 2, 4)
    return back.reshape(held, rows, cols)


def solution(mesh):
    placed = (P("scan", None, "col"), P(), P(), P(None, "col"))
    return jax.shard_map(
        body, mesh=mesh, in_specs=placed, out_specs=P("scan", None, "col"), check_vma=False
    )
```
